32 devices in a mesh: tm: 4 (over y, x), space: 8 (over z, core).
Axes of the slice: x: 2, y: 2, z: 4, core: 2. Of those that a mesh axis runs over, the one named last changes fastest.
Arguments:
- snapshots: bfloat16 [128, 256, 8192], P('tm', None, 'space'), may hold values from -6 to 6
- weights: float32 [8192], P('space'), may hold values from 6.1035156e-05 to 0.0009765625
Outputs:
- spectra: float32 [128, 128, 2, 128], P('space', 'tm')
The draws below stay inside these ranges and needn't reach their ends.
All inputs are finite; a program needn't handle non-finite values.
Results may differ from the reference program's by a relative error of at most 0.0027.
Values may be sent and summed in bfloat16 or wider, within the bound.
A program may use at most 192 MiB of HBM per device.

```python
import math
import jax
import jax.numpy as jnp
from jax import lax

NB = 128
NFFT = 256
NF = 128
X_DEV = 1024
XTOT = 8192
N_SPACE = 8


def shard_levels(key, dims, split, low, high):
    loudness, own = 1.0, jax.random.fold_in(key, 6)
    for position, parts in split:
        draws = jnp.exp(jax.random.uniform(jax.random.fold_in(own, position), (parts,), jnp.float32, low / len(split), high / len(split)))
        loudness = loudness * jnp.repeat(draws, dims[position] // parts).reshape([-1 if axis == position else 1 for axis in range(len(dims))])
    return loudness


def noise(own_key, shape, spread, limit, split=(), kind=jnp.bfloat16):
    result = jax.random.normal(own_key, shape, jnp.float32) * spread
    if len(split) > 0:
        result = shard_levels(own_key, shape, split, -0.22, 0.18) * result
    return jnp.clip(result, min=-limit, max=limit).astype(kind)


def setup_inputs(seed: int = 0) -> dict:
    key_of = jax.random.split(jax.random.key(seed), 3)
    snapshots = noise(key_of[0], (NB, NFFT, XTOT), 1.0, 6.0, ((0, 4), (2, 8)))
    weights = jnp.clip(jnp.exp(math.log(0.0009765625) - 2.7725887 * jax.random.uniform(key_of[1], (XTOT,), jnp.float32) ** shard_levels(key_of[1], (XTOT,), ((0, 8),), -0.2, 0.2)), 6.103515625e-05, 0.0009765625)
    return dict(snapshots=snapshots, weights=weights)


def make_table():
    steps_t = jnp.arange(NFFT, dtype=jnp.int32)
    freqs = jnp.arange(NF, dtype=jnp.int32)
    phase = (freqs[:, None] * steps_t[None, :] % NFFT).astype(jnp.float32) * (2.0 * math.pi / NFFT)
    hann = 0.5 - 0.5 * jnp.cos(steps_t.astype(jnp.float32) * (2.0 * math.pi / NFFT))
    factor = 1.0 / math.sqrt(3.0 * NFFT / 8.0)
    table = jnp.concatenate([jnp.cos(phase), -jnp.sin(phase)], axis=0) * hann[None, :] * factor
    return table.astype(jnp.bfloat16)

def reference(snapshots, weights):
    table = make_table().astype(jnp.float32)
    highest = lax.Precision.HIGHEST

    def accumulate(index, total):
        start = index * X_DEV
        block = lax.dynamic_slice_in_dim(snapshots, start, X_DEV, 2).astype(jnp.float32)
        scale = jnp.sqrt(lax.dynamic_slice_in_dim(weights, start, X_DEV, 0))
        coeffs = jnp.einsum('kt,btx->bkx', table, block, precision=highest) * scale[None, None, :]
        coeffs = coeffs.reshape(NB, 2, NF, X_DEV)
        real_part = jnp.einsum('acfx,bcfx->afb', coeffs, coeffs, precision=highest)
        imag_part = jnp.einsum('afx,bfx->afb', coeffs[:, 0], coeffs[:, 1], precision=highest) - jnp.einsum('afx,bfx->afb', coeffs[:, 1], coeffs[:, 0], precision=highest)
        return total + jnp.stack([real_part, imag_part], axis=2)
    start_total = jnp.zeros((NB, NF, 2, NB), jnp.float32)
    return lax.fori_loop(0, N_SPACE, accumulate, start_total)
```

```python
import functools
import math

import jax
import jax.numpy as jnp
import numpy as np
from jax import lax
from jax.experimental import pallas as pl
from jax.experimental.pallas import tpu as pltpu
from jax.sharding import PartitionSpec as P

MESH = pl.DeviceIdType.MESH
WIDTH = 128
GROUP = 16


def make_table(length, count):
    steps_t = np.arange(length, dtype=np.int32)
    freqs = np.arange(count, dtype=np.int32)
    turn = np.float32(2.0 * math.pi / length)
    phase = (freqs[:, None] * steps_t[None, :] % length).astype(np.float32) * turn
    hann = np.float32(0.5) - np.float32(0.5) * np.cos(steps_t.astype(np.float32) * turn)
    factor = np.float32(1.0 / math.sqrt(3.0 * length / 8.0))
    table = np.concatenate([np.cos(phase), -np.sin(phase)], axis=0) * hann[None, :] * factor
    return jnp.asarray(table.astype(jnp.bfloat16))


def swap_matrix():
    size = GROUP * GROUP
    source = np.arange(size).reshape(GROUP, GROUP).T.reshape(-1)
    return jnp.asarray(np.eye(size, dtype=np.float32)[source].astype(jnp.bfloat16))


def order_matrix(unit_size, blocks, n_space):
    size = unit_size * 2 * blocks
    rows = blocks // n_space
    source = np.arange(size).reshape(unit_size, 2, n_space, rows).transpose(2, 0, 1, 3).reshape(-1)
    return jnp.asarray(np.eye(size, dtype=np.float32)[source].astype(jnp.bfloat16))


def partner(me, k, count):
    if count & (count - 1):
        return lax.rem(me + k, count)
    other, bit = 0, 1
    while bit < count:
        have = lax.rem(lax.div(me, bit), 2)
        other = other + bit * (1 - have if k & bit else have)
        bit *= 2
    return other


def signal(sem, where):
    pl.semaphore_signal(sem, inc=1, device_id=where, device_id_type=MESH)


def kernel(
    n_tm, n_space, width, early, unit_size, later,
    x_ref, w_hbm, table_hbm, swap_hbm, order_hbm, out_buf,
    w_ref, table_ref, swap_ref, order_ref,
    x_buf, rows_buf, outgoing, owned, part, arrived,
    const_sem, x_sem, early_send, early_recv, unit_send, unit_recv, sum_send, sum_recv,
    relay_sem, up_sem, down_sem,
):
    me = lax.axis_index("tm")
    seat = lax.axis_index("space")
    blocks, length, points = x_ref.shape
    half = length // 2
    freqs = half // n_tm
    tiles = points // width
    steps = blocks // GROUP * tiles
    units = freqs // unit_size
    total = blocks * n_tm
    rows = total // n_space
    slab = unit_size * 2 * rows
    peers = list(range(n_tm - 1, 0, -1))
    near = [k for k in peers if k & (k - 1) == 0]
    far = [k for k in peers if k & (k - 1)]
    seats = list(range(n_space - 1, 0, -1))

    def place(step):
        start = pl.multiple_of(step // tiles * GROUP, GROUP)
        return start, pl.multiple_of(step % tiles * width, width)

    def load(step):
        start, column = place(step)
        return pltpu.make_async_copy(
            x_ref.at[pl.ds(start, GROUP), :, pl.ds(column, width)],
            x_buf.at[step % 2],
            x_sem.at[step % 2],
        )

    def early_copy(step, k):
        start, column = place(step)
        return pltpu.make_async_remote_copy(
            src_ref=outgoing.at[k - 1, pl.ds(0, early), :, pl.ds(start, GROUP), pl.ds(column, width)],
            dst_ref=owned.at[
                pl.ds(0, early), :, pl.ds(pl.multiple_of(me * blocks + start, GROUP), GROUP), pl.ds(column, width)
            ],
            send_sem=early_send.at[step, k - 1],
            recv_sem=early_recv.at[step, k - 1],
            device_id={"tm": partner(me, k, n_tm)},
            device_id_type=MESH,
        )

    def later_copy(item, k):
        first, size, column, span = later[item]
        columns = pl.ds(column, span)
        return pltpu.make_async_remote_copy(
            src_ref=outgoing.at[k - 1, pl.ds(first, size), :, :, columns],
            dst_ref=owned.at[pl.ds(first, size), :, pl.ds(pl.multiple_of(me * blocks, GROUP), blocks), columns],
            send_sem=unit_send.at[item, k - 1],
            recv_sem=unit_recv.at[item, k - 1],
            device_id={"tm": partner(me, k, n_tm)},
            device_id_type=MESH,
        )

    def sum_copy(unit, k):
        owner = partner(seat, k, n_space)
        return pltpu.make_async_remote_copy(
            src_ref=part.at[unit, owner],
            dst_ref=arrived.at[unit, k - 1],
            send_sem=sum_send.at[unit],
            recv_sem=sum_recv.at[unit],
            device_id={"space": owner},
            device_id_type=MESH,
        )

    constants = [
        pltpu.make_async_copy(pair[0], pair[1], const_sem.at[i])
        for i, pair in enumerate(
            [(table_hbm, table_ref), (w_hbm, w_ref), (swap_hbm, swap_ref), (order_hbm, order_ref)]
        )
    ]
    constants[0].start()
    constants[1].start()
    load(0).start()
    constants[2].start()
    constants[3].start()
    bits = [1 << i for i in range(n_tm.bit_length() - 1)]
    has_left = jnp.where(seat > 0, 1, 0)
    has_right = jnp.where(seat < n_space - 1, 1, 0)
    barrier = pltpu.get_barrier_semaphore()
    for k in bits:
        signal(barrier, {"tm": partner(me, k, n_tm)})

    @pl.when(seat > 0)
    def _():
        signal(barrier, {"space": seat - 1})

    @pl.when(seat < n_space - 1)
    def _():
        signal(barrier, {"space": seat + 1})

    for copy in constants:
        copy.wait()

    def transform(step, carry):
        start, column = place(step)

        @pl.when(step + 1 < steps)
        def _():
            load(step + 1).start()

        load(step).wait()
        scale = jnp.sqrt(w_ref[:, pl.ds(column, width)])

        for b in range(0, GROUP, 2):
            pair = jnp.concatenate([x_buf[step % 2, b], x_buf[step % 2, b + 1]], axis=1)
            product = jnp.dot(table_ref[...], pair, preferred_element_type=jnp.float32)
            rows_buf[b] = (product[:, :width] * scale).astype(jnp.bfloat16)
            rows_buf[b + 1] = (product[:, width:] * scale).astype(jnp.bfloat16)

        def exchange(k, f):
            target = owned if k == 0 else outgoing.at[k - 1]
            base = partner(me, k, n_tm) * freqs
            offset = me * blocks + start if k == 0 else start
            for c in range(2):
                row = pl.multiple_of(c * half + base + f, GROUP)
                taken = rows_buf[:, pl.ds(row, GROUP), :].reshape(GROUP * GROUP, width)
                swapped = jnp.dot(swap_ref[...], taken, preferred_element_type=jnp.float32)
                target[
                    pl.ds(f, GROUP), c, pl.ds(pl.multiple_of(offset, GROUP), GROUP), pl.ds(column, width)
                ] = swapped.astype(jnp.bfloat16).reshape(GROUP, GROUP, width)

        starts = range(0, freqs, GROUP)
        first = [(k, f) for f in starts if f < early for k in peers]
        rest = [(k, f) for f in starts if f >= early for k in peers] + [(0, f) for f in starts]
        for k, f in first:
            exchange(k, f)

        @pl.when(step == 0)
        def _():
            pl.semaphore_wait(barrier, len(bits) + has_left + has_right)
            for i, k in enumerate(bits[1:]):
                signal(relay_sem.at[i], {"tm": partner(me, k, n_tm)})

        for k in near:
            early_copy(step, k).start()

        for k, f in rest:
            exchange(k, f)

        @pl.when(step == 0)
        def _():
            for i, k in enumerate(bits[1:]):
                pl.semaphore_wait(relay_sem.at[i], 1)

        for k in far:
            early_copy(step, k).start()

        return carry

    lax.fori_loop(0, steps, transform, 0)

    for item in range(len(later)):
        for k in peers:
            later_copy(item, k).start()

    @pl.when(seat > 0)
    def _():
        pl.semaphore_wait(up_sem, 1)

    @pl.when(seat < n_space - 1)
    def _():
        signal(up_sem, {"space": seat + 1})
        pl.semaphore_wait(down_sem, 1)

    @pl.when(seat > 0)
    def _():
        signal(down_sem, {"space": seat - 1})

    def early_wait(step, carry):
        for k in range(1, n_tm):
            early_copy(step, k).wait()
        return carry

    lax.fori_loop(0, steps, early_wait, 0)

    def finish(unit):
        pltpu.make_async_copy(arrived.at[unit], arrived.at[unit], sum_recv.at[unit]).wait()
        value = part[unit, seat].astype(jnp.float32)
        for k in range(n_space - 1):
            value = value + arrived[unit, k].astype(jnp.float32)
        for i in range(2 * unit_size):
            out_buf[:, pl.ds(unit * 2 * unit_size + i, 1), :] = value[i * rows : (i + 1) * rows][:, None, :]

    def cross(unit, carry):
        for item in range(len(later) - 1):

            @pl.when(unit == later[item][0] // unit_size)
            def _(item=item):
                for k in peers:
                    later_copy(item, k).wait_recv()

        pieces = []
        grams = []
        for column in (0, points // 2):
            if column:

                @pl.when(unit == units - 1)
                def _():
                    for k in peers:
                        later_copy(len(later) - 1, k).wait_recv()

            for i in range(unit_size):
                both = owned[unit * unit_size + i, :, :, pl.ds(column, points // 2)]
                both = both.reshape(2 * total, points // 2)
                grams.append(
                    lax.dot_general(both, both, (((1,), (1,)), ((), ())), preferred_element_type=jnp.float32)
                )
        for i in range(unit_size):
            gram = grams[i] + grams[unit_size + i]
            pieces.append(gram[:total, :total] + gram[total:, total:])
            pieces.append(gram[:total, total:] - gram[total:, :total])
        pieces = [piece.astype(jnp.bfloat16) for piece in pieces]
        if rows % GROUP == 0:
            for i, piece in enumerate(pieces):
                for d in range(n_space):
                    part[unit, d, i * rows : (i + 1) * rows, :] = piece[d * rows : (d + 1) * rows]
        else:
            ordered = jnp.dot(
                order_ref[...], jnp.concatenate(pieces, axis=0), preferred_element_type=jnp.float32
            )
            part[unit] = ordered.astype(jnp.bfloat16).reshape(n_space, slab, total)

        for k in seats:
            sum_copy(unit, k).start()

        @pl.when(unit > 1)
        def _():
            finish(unit - 2)

        return carry

    lax.fori_loop(0, units, cross, 0)
    for unit in (units - 2, units - 1):
        finish(unit)

    def sent(unit, carry):
        pltpu.make_async_copy(arrived.at[unit], arrived.at[unit], sum_send.at[unit]).wait()
        return carry

    lax.fori_loop(0, units, sent, 0)
    for item in range(len(later)):
        for k in peers:
            later_copy(item, k).wait_send()


def per_device(n_tm, n_space, snapshots, weights):
    blocks, length, points = snapshots.shape
    total, freqs = blocks * n_tm, length // 2 // n_tm
    rows = total // n_space
    unit_size = max(1, GROUP // (2 * rows))
    units = freqs // unit_size
    slab = unit_size * 2 * rows
    width = min(WIDTH, points)
    early = max(freqs // 4, unit_size)
    later, first = [], early
    while first + unit_size < freqs:
        size = max(unit_size, (freqs - first) // (2 * unit_size) * unit_size)
        later.append((first, size, 0, points))
        first += size
    later += [(first, unit_size, column, points // 2) for column in (0, points // 2)]
    steps = blocks // GROUP * (points // width)
    hbm = pl.BlockSpec(memory_space=pl.ANY)
    bf16 = jnp.bfloat16
    table = make_table(length, length // 2)
    swap = swap_matrix()
    order = swap if rows % GROUP == 0 else order_matrix(unit_size, total, n_space)
    sums = pl.pallas_call(
        functools.partial(kernel, n_tm, n_space, width, early, unit_size, later),
        out_shape=jax.ShapeDtypeStruct((rows, freqs * 2, total), jnp.float32),
        in_specs=[hbm] * 5,
        out_specs=pl.BlockSpec(memory_space=pltpu.VMEM),
        scratch_shapes=[
            pltpu.VMEM((1, points), jnp.float32),
            pltpu.VMEM(table.shape, bf16),
            pltpu.VMEM(swap.shape, bf16),
            pltpu.VMEM(order.shape, bf16),
            pltpu.VMEM((2, GROUP, length, width), bf16),
            pltpu.VMEM((GROUP, length, width), bf16),
            pltpu.VMEM((n_tm - 1, freqs, 2, blocks, points), bf16),
            pltpu.VMEM((freqs, 2, total, points), bf16),
            pltpu.VMEM((units, n_space, slab, total), bf16),
            pltpu.VMEM((units, n_space - 1, slab, total), bf16),
            pltpu.SemaphoreType.DMA((4,)),
            pltpu.SemaphoreType.DMA((2,)),
            pltpu.SemaphoreType.DMA((steps, n_tm - 1)),
            pltpu.SemaphoreType.DMA((steps, n_tm - 1)),
            pltpu.SemaphoreType.DMA((len(later), n_tm - 1)),
            pltpu.SemaphoreType.DMA((len(later), n_tm - 1)),
            pltpu.SemaphoreType.DMA((units,)),
            pltpu.SemaphoreType.DMA((units,)),
            pltpu.SemaphoreType.REGULAR((max(1, n_tm.bit_length() - 2),)),
            pltpu.SemaphoreType.REGULAR,
            pltpu.SemaphoreType.REGULAR,
        ],
        compiler_params=pltpu.CompilerParams(
            collective_id=0, has_side_effects=True, vmem_limit_bytes=60 * 1024 * 1024
        ),
    )(
        snapshots,
        weights[None, :],
        table,
        swap,
        order,
    )
    return sums.reshape(rows, freqs, 2, total)


def solution(mesh):
    return jax.shard_map(
        functools.partial(per_device, mesh.shape["tm"], mesh.shape["space"]),
        mesh=mesh,
        in_specs=(P("tm", None, "space"), P("space")),
        out_specs=P("space", "tm", None, None),
        check_vma=False,
    )
```
